256 devices in a mesh: ctx: 16 (over y_hi, x, core), dp: 16 (over y_lo, z).
Axes of the slice: x: 4, y: 4 (y_hi: 2, y_lo: 2; y = y_hi * 2 + y_lo), z: 8, core: 2. Of those that a mesh axis runs over, the one named last changes fastest.
Arguments:
- queries: bfloat16 [16, 2048, 1536], P('dp', 'ctx'), as said below
- keys: bfloat16 [16, 2048, 1536], P('dp', 'ctx'), as said below
- values: bfloat16 [16, 2048, 1536], P('dp', 'ctx'), may hold values from -6 to 6
- tangent_queries: bfloat16 [16, 2048, 1536], P('dp', 'ctx'), may hold values from -6 to 6
- tangent_keys: bfloat16 [16, 2048, 1536], P('dp', 'ctx'), may hold values from -6 to 6
- tangent_values: bfloat16 [16, 2048, 1536], P('dp', 'ctx'), may hold values from -6 to 6
- clip_ids: int32 [16, 2048], P('dp', 'ctx'), may hold values from 0 to 3, never falling along the last dimension, each value on 1 to 1024 neighbouring positions
- block_order: int32 [16], replicated, may hold values from 0 to 15, each once
- out_weight: bfloat16 [1536, 3072], replicated, may hold values from -0.15625 to 0.15625
- layer_scale: float32 [3072], replicated, may hold values from 0.1 to 1.9
- cotangent: bfloat16 [16, 2048, 3072], P('dp', 'ctx'), as said below
Outputs:
- tangent_branch: bfloat16 [16, 2048, 3072], P('dp', 'ctx')
- scale_grad: float32 [3072], replicated
The draws below stay inside these ranges and needn't reach their ends.
Inputs may be any that keep to these rules, and one draw needn't show every extreme that they name: `clip_ids`: ids never fall along a sample's rows; each of the 4 clips is a run of consecutive rows. `block_order`: each block number appears once. `queries`: real-valued. `keys`: real-valued. `cotangent`: real-valued.
All inputs are finite; a program needn't handle non-finite values.
Results may differ from the reference program's by a relative error of at most 0.02.
The reference program's roundings to bfloat16 on the way count: a program that leaves them out, or rounds other values in their place, can miss the bound.
Values may be sent and summed in bfloat16 or wider, within the bound.
A program may use at most 192 MiB of HBM per device.

```python
import math
import jax
import jax.numpy as jnp
import numpy as np
from jax import lax

D = 3072
HEADS = 12
HD = 128
TOK_DEV = 128
CLIPS = 4
HW = 1536
SEQ = 2048
SAMPLES = 16
N_CTX = 16


def qk_draw(key, which):
    noise = jax.random.normal(jax.random.fold_in(key, 101 + which), (SAMPLES, SEQ, HEADS * HD), jnp.float32)
    return noise.astype(jnp.bfloat16)


def draw_queries(key, part):
    return qk_draw(key, 0)


def draw_keys(key, part):
    return qk_draw(key, 1)


def draw_cotangent(key, part):
    noise = jax.random.normal(jax.random.fold_in(key, 301), (SAMPLES, SEQ, D), jnp.float32)
    row_scale = jnp.exp(jax.random.uniform(jax.random.fold_in(key, 302), (SAMPLES, SEQ, 1), jnp.float32, 0.0, math.log(10.0)))
    col_scale = jnp.exp(jax.random.uniform(jax.random.fold_in(key, 303), (1, 1, D), jnp.float32, 0.0, math.log(10.0)))
    along_seq = 1.0 + 2.0 * jnp.arange(SEQ, dtype=jnp.float32) / SEQ
    along_samples = 1.0 + 2.0 * jnp.arange(SAMPLES, dtype=jnp.float32) / max(SAMPLES - 1, 1)
    rising = along_samples[:, None, None] * along_seq[None, :, None]
    return (noise * row_scale * col_scale * rising / 30.0).astype(jnp.bfloat16)


def block_scale(stream_key, dims, shards, low, top_value):
    loudness, own = 1.0, jax.random.fold_in(stream_key, 6)
    for axis_at, shards_of in shards:
        draws = jnp.exp(jax.random.uniform(jax.random.fold_in(own, axis_at), (shards_of,), jnp.float32, low / len(shards), top_value / len(shards)))
        loudness = loudness * jnp.repeat(draws, dims[axis_at] // shards_of).reshape([-1 if axis == axis_at else 1 for axis in range(len(dims))])
    return loudness


def split_up(number_of, total, reach, slope):
    weights = [(1 << 20) // math.isqrt(rank ** slope) + 1 for rank in range(2, number_of + 1)]
    rest, counts = total - reach - (number_of - 1), [1] * (number_of - 1)
    while rest > 0:
        movable = [i for i in range(number_of - 1) if counts[i] < reach]
        pool, left = sum([weights[i] for i in movable]), rest
        for i in movable:
            addition = min(reach - counts[i], max(1, left * weights[i] // pool), rest)
            counts[i] = counts[i] + addition
            rest = rest - addition
    return np.array([reach] + counts)


def uneven(rng, count, total, reach, lean):
    if count == 2:
        one = jax.random.randint(rng, (), max(1, total - reach), min(reach, total - 1) + 1)
        return jnp.stack([one, total - one])
    tallies = jnp.asarray(split_up(count, total, reach, lean), jnp.int32)
    couples = (count - 1) // 2
    donor, receiver = tallies[1:1 + 2 * couples:2], tallies[2:2 + 2 * couples:2]
    slack = jnp.minimum(donor - 1, reach - receiver)
    moved = jax.random.randint(jax.random.fold_in(rng, 1), (couples,), 0, 1 << 20) % (slack + 1)
    tallies = tallies.at[1:1 + 2 * couples:2].set(donor - moved).at[2:2 + 2 * couples:2].set(receiver + moved)
    return tallies[jax.random.permutation(jax.random.fold_in(rng, 2), count)]


def bell_draw(own_key, dims, scale, bound, cuts=(), held_as=jnp.bfloat16):
    values = jax.random.normal(own_key, dims, jnp.float32) * scale
    if len(cuts) > 0:
        values = block_scale(own_key, dims, cuts, -0.22, 0.18) * values
    return jnp.clip(values, min=-bound, max=bound).astype(held_as)


def setup_inputs(seed: int = 0) -> dict:
    seeds = jax.random.split(jax.random.key(seed), 12)
    queries = draw_queries(jax.random.fold_in(seeds[11], 71), 0)
    keys = draw_keys(jax.random.fold_in(seeds[11], 71), 0)
    values = bell_draw(seeds[2], (SAMPLES, SEQ, HW), 1.0, 6.0, ((0, 16), (1, 16)))
    tangent_queries = bell_draw(seeds[3], (SAMPLES, SEQ, HW), 1.0, 6.0, ((0, 16), (1, 16)))
    tangent_keys = bell_draw(seeds[4], (SAMPLES, SEQ, HW), 1.0, 6.0, ((0, 16), (1, 16)))
    tangent_values = bell_draw(seeds[5], (SAMPLES, SEQ, HW), 1.0, 6.0, ((0, 16), (1, 16)))
    clip_ids = jax.vmap(lambda own: jnp.searchsorted(jnp.cumsum(uneven(own, CLIPS, SEQ, SEQ // 2, 2)), jnp.arange(SEQ), side="right"))(jax.random.split(seeds[6], SAMPLES)).reshape((SAMPLES, SEQ)).astype(jnp.int32)
    block_order = jax.random.permutation(seeds[7], N_CTX).astype(jnp.int32)
    out_weight = bell_draw(seeds[8], (HW, D), HW ** -0.5, 0.15625)
    layer_scale = jnp.clip(1.0 + 0.18 * jax.random.normal(seeds[9], (D,), jnp.float32), 0.1, 1.9)
    cotangent = draw_cotangent(jax.random.fold_in(seeds[11], 71), 0)
    return {"queries": queries, "keys": keys, "values": values, "tangent_queries": tangent_queries, "tangent_keys": tangent_keys, "tangent_values": tangent_values, "clip_ids": clip_ids, "block_order": block_order, "out_weight": out_weight, "layer_scale": layer_scale, "cotangent": cotangent}


def rotate(x, pos, half_dim):
    frequency = 10000.0 ** (-jnp.arange(half_dim, dtype=jnp.float32) / half_dim)
    angles = pos.astype(jnp.float32)[:, None] * frequency[None, :]
    cosine = jnp.cos(angles)[:, None, :]
    sine_part = jnp.sin(angles)[:, None, :]
    front_part = x[..., :half_dim]
    back_part = x[..., half_dim:]
    return jnp.concatenate([front_part * cosine - back_part * sine_part, back_part * cosine + front_part * sine_part], axis=-1)

def reference(queries, keys, values, tangent_queries, tangent_keys, tangent_values, clip_ids, block_order, out_weight, layer_scale, cotangent):
    seq_len = queries.shape[1]
    heads = HEADS
    head_dim = HD
    scale = head_dim ** (-0.5)
    positions = (block_order[:, None] * TOK_DEV + jnp.arange(TOK_DEV, dtype=jnp.int32)[None, :]).reshape(-1).astype(jnp.int32)

    def heads_first(x, turned):
        y = x.reshape(seq_len, heads, head_dim)
        if turned:
            y = rotate(y.astype(jnp.float32), positions, head_dim // 2).astype(jnp.bfloat16)
        return jnp.transpose(y, (1, 0, 2))

    def one_sample(items):
        query_s, key_s, value_s, tquery_s, tkey_s, tvalue_s, ids_s, cot_s = items
        same_clip = ids_s[:, None] == ids_s[None, :]

        def one_head(head_items):
            qh, kh, vh, tqh, tkh, tvh = head_items
            scores = jnp.dot(qh, kh.T, preferred_element_type=jnp.float32) * scale
            scores = jnp.where(same_clip, scores, -jnp.inf)
            slopes = (jnp.dot(tqh, kh.T, preferred_element_type=jnp.float32) + jnp.dot(qh, tkh.T, preferred_element_type=jnp.float32)) * scale
            best = lax.optimization_barrier(jnp.max(scores, axis=1, keepdims=True))
            weights = jnp.exp(scores - best)
            tilted = weights * slopes
            total = lax.optimization_barrier(jnp.sum(weights, axis=1, keepdims=True))
            weighted = lax.optimization_barrier(jnp.sum(tilted, axis=1, keepdims=True))
            weights_b = weights.astype(jnp.bfloat16)
            tilted_b = tilted.astype(jnp.bfloat16)
            primal = jnp.dot(weights_b, vh, preferred_element_type=jnp.float32)
            slope_part = jnp.dot(tilted_b, vh, preferred_element_type=jnp.float32)
            spread = jnp.dot(weights_b, tvh, preferred_element_type=jnp.float32)
            mean_out = primal / total
            return ((slope_part + spread) / total - weighted / total * mean_out).astype(jnp.bfloat16)
        head_outs = lax.map(one_head, (heads_first(query_s, True), heads_first(key_s, True), heads_first(value_s, False), heads_first(tquery_s, True), heads_first(tkey_s, True), heads_first(tvalue_s, False)))
        rows = jnp.transpose(head_outs, (1, 0, 2)).reshape(seq_len, heads * head_dim)
        projected = jnp.dot(rows, out_weight, preferred_element_type=jnp.float32)
        branch = (layer_scale * projected).astype(jnp.bfloat16)
        return (branch, lax.optimization_barrier(jnp.sum(cot_s.astype(jnp.float32) * projected, axis=0)))
    branch, partial_grad = lax.map(one_sample, (queries, keys, values, tangent_queries, tangent_keys, tangent_values, clip_ids, cotangent))
    return (branch, lax.optimization_barrier(jnp.sum(partial_grad, axis=0)) / math.sqrt(SAMPLES * seq_len))
```

```python
import math

import jax
import jax.numpy as jnp
import numpy as np
from jax import lax
from jax.experimental import pallas as pl
from jax.experimental.pallas import tpu as pltpu
from jax.sharding import PartitionSpec as P

MESH = pl.DeviceIdType.MESH
HEADS = 12
HD = 128
ROWS = 128
F32 = jnp.float32
BF16 = jnp.bfloat16


def owner_of(head):
    row, rest = head // 6, head % 6
    return 8 * row + rest + (rest + 2 * row) // 3


def kernel(
    n_ctx,
    n_dp,
    order_ref,
    q_ref,
    k_ref,
    v_ref,
    tq_ref,
    tk_ref,
    tv_ref,
    ids_ref,
    turn_ref,
    block_turn_ref,
    w_ref,
    ls_ref,
    cot_ref,
    branch_ref,
    grad_ref,
    kk_stage,
    qq_stage,
    id_stage,
    kk,
    vv,
    qq,
    id_rows,
    id_cols,
    s_buf,
    wb_buf,
    tb_buf,
    out_stage,
    attn,
    w_buf,
    g_part,
    g_ctx,
    g_sum,
    g_dp,
    w_sem,
    send_k,
    send_v,
    send_tv,
    send_q,
    send_id,
    recv_k,
    recv_v,
    recv_q,
    recv_id,
    send_out,
    recv_out,
    send_gc,
    recv_gc,
    send_gd,
    recv_gd,
):
    me = lax.axis_index("ctx")
    me_dp = lax.axis_index("dp")
    chip, core = me // 2, me % 2
    row, col = chip // 4, chip % 4
    my_head = 6 * row + (3 * col + 1 - row) // 2 + core
    is_owner = core * ((row + col) % 2) == 0
    chips = n_ctx // 2

    w_copy = pltpu.make_async_copy(w_ref, w_buf, w_sem)
    w_copy.start()

    barrier = pltpu.get_barrier_semaphore()

    @pl.loop(1, n_ctx)
    def _(i):
        pl.semaphore_signal(
            barrier, inc=1, device_id={"ctx": (me + i) % n_ctx}, device_id_type=MESH
        )

    @pl.loop(1, n_dp)
    def _(i):
        pl.semaphore_signal(
            barrier, inc=1, device_id={"dp": (me_dp + i) % n_dp}, device_id_type=MESH
        )

    place = order_ref[me]
    cos_b = block_turn_ref[0, pl.ds(place, 1), :]
    sin_b = block_turn_ref[1, pl.ds(place, 1), :]
    cos_t, sin_t = turn_ref[0], turn_ref[1]
    lane = lax.broadcasted_iota(jnp.int32, (ROWS, HD), 1)
    cosine = cos_b * cos_t - sin_b * sin_t
    sine = sin_b * cos_t + cos_b * sin_t
    sine = jnp.where(lane < HD // 2, -sine, sine)

    def turned(x, c, s):
        x = x.astype(F32)
        return (x * c + pltpu.roll(x, HD // 2, axis=1) * s).astype(BF16)

    for h in range(HEADS):
        cols = slice(h * HD, (h + 1) * HD)
        kk_stage[h, :, 0:HD] = turned(k_ref[0, :, cols], cosine, sine)
        kk_stage[h, :, HD : 2 * HD] = turned(tk_ref[0, :, cols], cosine, sine)
    cosine, sine = cosine * 0.0625, sine * 0.0625
    for h in range(HEADS):
        cols = slice(h * HD, (h + 1) * HD)
        qq_stage[h, :, 0:HD] = turned(tq_ref[0, :, cols], cosine, sine)
        qq_stage[h, :, HD : 2 * HD] = turned(q_ref[0, :, cols], cosine, sine)
    id_stage[...] = jnp.broadcast_to(ids_ref[...].astype(F32), (8, HD))

    pl.semaphore_wait(barrier, n_ctx - 1 + n_dp - 1)

    rows_here = pl.ds(pl.multiple_of(me * ROWS, ROWS), ROWS)

    def pieces(h):
        cols = pl.ds(pl.multiple_of(h * HD, HD), HD)
        return [
            (id_stage, id_rows.at[me], send_id.at[h], recv_id),
            (kk_stage.at[h], kk.at[rows_here, :], send_k.at[h], recv_k),
            (v_ref.at[0, :, cols], vv.at[rows_here, pl.ds(0, HD)], send_v.at[h], recv_v),
            (tv_ref.at[0, :, cols], vv.at[rows_here, pl.ds(HD, HD)], send_tv.at[h], recv_v),
            (qq_stage.at[h], qq.at[rows_here, :], send_q.at[h], recv_q.at[me]),
        ]

    def remote(piece, to):
        src, dst, ssem, rsem = piece
        return pltpu.make_async_remote_copy(
            src_ref=src,
            dst_ref=dst,
            send_sem=ssem,
            recv_sem=rsem,
            device_id={"ctx": to},
            device_id_type=MESH,
        )

    def start_sends(which):
        @pl.loop(0, HEADS)
        def _(i):
            h = (i + my_head) % HEADS
            to = owner_of(h)

            @pl.when(to != me)
            def _():
                for p in which:
                    remote(pieces(h)[p], to).start()

            @pl.when(to == me)
            def _():
                for p in which:
                    src, dst, _, rsem = pieces(h)[p]
                    pltpu.make_async_copy(src, dst, rsem).start()

    start_sends((0, 1, 2, 3))
    start_sends((4,))

    @pl.when(is_owner)
    def _():
        pltpu.make_async_copy(id_rows, id_rows, recv_id).wait()

        @pl.loop(0, n_ctx)
        def _(j):
            ids = jnp.broadcast_to(id_rows[j, 0:1, :], (ROWS, HD))
            id_cols[pl.ds(pl.multiple_of(j * ROWS, ROWS), ROWS), :] = ids.T

        pltpu.make_async_copy(kk, kk, recv_k).wait()
        pltpu.make_async_copy(vv, vv, recv_v).wait()

        tile = 2 * ROWS
        step = math.log2(math.e) * math.sqrt(2.0)
        contract_last = (((1,), (1,)), ((), ()))

        @pl.loop(0, chips)
        def _(t):
            at = (chip + t) % chips
            rows = pl.ds(pl.multiple_of(at * tile, tile), tile)
            for c in range(2):
                block = at * 2 + c
                part = qq.at[pl.ds(pl.multiple_of(block * ROWS, ROWS), ROWS), :]
                pltpu.make_async_copy(part, part, recv_q.at[block]).wait()
            both = qq[rows, :]
            q = both[:, HD : 2 * HD]
            mine = id_cols[rows, :]
            best = jnp.full((tile, HD), -jnp.inf, F32)
            for c in range(chips):
                keys = kk[c * tile : (c + 1) * tile, 0:HD]
                s = lax.dot_general(q, keys, contract_last, preferred_element_type=F32)
                for half in range(2):
                    j = 2 * c + half
                    theirs = jnp.broadcast_to(id_rows[j, 0:1, :], (tile, HD))
                    s_half = jnp.where(mine == theirs, s[:, half * HD : (half + 1) * HD], -jnp.inf)
                    s_buf[:, j * HD : (j + 1) * HD] = s_half
                    best = jnp.maximum(best, s_half)
            best = jnp.broadcast_to(jnp.max(best, axis=1, keepdims=True), (tile, HD))
            total = jnp.zeros((tile, HD), F32)
            weighted = jnp.zeros((tile, HD), F32)
            for c in range(chips):
                keys = kk[c * tile : (c + 1) * tile, :]
                slopes = lax.dot_general(both, keys, contract_last, preferred_element_type=F32)
                for half in range(2):
                    j = 2 * c + half
                    there = slice(j * HD, (j + 1) * HD)
                    w = jnp.exp2((s_buf[:, there] - best) * step)
                    tilted = w * slopes[:, half * HD : (half + 1) * HD]
                    total = total + w
                    weighted = weighted + tilted
                    wb_buf[:, there] = w.astype(BF16)
                    tb_buf[:, there] = tilted.astype(BF16)
            sums = jnp.dot(wb_buf[...], vv[...], preferred_element_type=F32)
            slope_part = jnp.dot(tb_buf[...], vv[:, 0:HD], preferred_element_type=F32)
            total = jnp.sum(total, axis=1, keepdims=True)
            weighted = jnp.sum(weighted, axis=1, keepdims=True) * math.sqrt(2.0)
            primal, spread = sums[:, 0:HD], sums[:, HD : 2 * HD]
            result = (slope_part * math.sqrt(2.0) + spread) / total - (weighted / total) * (
                primal / total
            )
            out_stage[at] = result.astype(BF16)
            for c in range(2):
                block = at * 2 + c
                src = out_stage.at[at, pl.ds(c * ROWS, ROWS), :]
                dst = attn.at[:, pl.ds(pl.multiple_of(my_head * HD, HD), HD)]

                @pl.when(block != me)
                def _():
                    remote((src, dst, send_out.at[block], recv_out), block).start()

                @pl.when(block == me)
                def _():
                    pltpu.make_async_copy(src, dst, recv_out).start()

    w_copy.wait()
    pltpu.make_async_copy(attn, attn, recv_out).wait()

    width = w_buf.shape[1]
    wide = width // 8
    for n in range(8):
        cols = slice(n * wide, (n + 1) * wide)
        projected = jnp.dot(attn[...], w_buf[:, cols], preferred_element_type=F32)
        branch_ref[0, :, cols] = (ls_ref[:, cols] * projected).astype(BF16)
        weighed = cot_ref[0, :, cols].astype(F32) * projected
        g_part[n : n + 1, :] = jnp.sum(weighed, axis=0, keepdims=True)

    def exchange(axis, index, size, src, dst, ssem, rsem):
        def copy_to(i):
            return pltpu.make_async_remote_copy(
                src_ref=src,
                dst_ref=dst.at[index],
                send_sem=ssem.at[i],
                recv_sem=rsem,
                device_id={axis: (index + i) % size},
                device_id_type=MESH,
            )

        @pl.loop(1, size)
        def _(i):
            copy_to(i).start()

        pltpu.make_async_copy(src, dst.at[index], rsem).start()
        pltpu.make_async_copy(dst, dst, rsem).wait()
        return copy_to

    copy_c = exchange("ctx", me, n_ctx, g_part, g_ctx, send_gc, recv_gc)
    acc = g_ctx[0]
    for i in range(1, n_ctx):
        acc = acc + g_ctx[i]
    g_sum[...] = acc
    copy_d = exchange("dp", me_dp, n_dp, g_sum, g_dp, send_gd, recv_gd)
    acc = g_dp[0]
    for i in range(1, n_dp):
        acc = acc + g_dp[i]
    acc = acc / math.sqrt(n_ctx * n_dp * ROWS)
    for n in range(8):
        grad_ref[:, n * wide : (n + 1) * wide] = acc[n : n + 1, :]

    @pl.loop(0, HEADS)
    def _(h):
        to = owner_of(h)

        @pl.when(to != me)
        def _():
            for piece in pieces(h):
                remote(piece, to).wait_send()

    @pl.when(is_owner)
    def _():
        @pl.loop(0, n_ctx)
        def _(block):
            @pl.when(block != me)
            def _():
                src = out_stage.at[block // 2, pl.ds((block % 2) * ROWS, ROWS), :]
                dst = attn.at[:, pl.ds(pl.multiple_of(my_head * HD, HD), HD)]
                remote((src, dst, send_out.at[block], recv_out), block).wait_send()

    @pl.loop(1, n_ctx)
    def _(i):
        copy_c(i).wait_send()

    @pl.loop(1, n_dp)
    def _(i):
        copy_d(i).wait_send()


def turn_tables(blocks):
    frequency = 10000.0 ** (-np.arange(HD // 2, dtype=np.float64) / (HD // 2))
    frequency = np.concatenate([frequency, frequency])
    inside = np.arange(ROWS, dtype=np.float64)[:, None] * frequency
    start = ROWS * np.arange(blocks, dtype=np.float64)[:, None] * frequency
    return (
        np.stack([np.cos(inside), np.sin(inside)]).astype(np.float32),
        np.stack([np.cos(start), np.sin(start)]).astype(np.float32),
    )


def solution(mesh):
    n_ctx, n_dp = mesh.shape["ctx"], mesh.shape["dp"]
    inside, start = turn_tables(n_ctx)

    def local(
        queries,
        keys,
        values,
        tangent_queries,
        tangent_keys,
        tangent_values,
        clip_ids,
        block_order,
        out_weight,
        layer_scale,
        cotangent,
    ):
        width = out_weight.shape[1]
        seq = n_ctx * ROWS
        tile = 2 * ROWS
        vmem = pl.BlockSpec(memory_space=pltpu.VMEM)
        anywhere = pl.BlockSpec(memory_space=pl.ANY)
        dma = pltpu.SemaphoreType.DMA
        branch, grad = pl.pallas_call(
            lambda *refs: kernel(n_ctx, n_dp, *refs),
            out_shape=(
                jax.ShapeDtypeStruct((1, ROWS, width), BF16),
                jax.ShapeDtypeStruct((1, width), F32),
            ),
            in_specs=[
                pl.BlockSpec(memory_space=pltpu.SMEM),
                vmem,
                vmem,
                anywhere,
                vmem,
                vmem,
                anywhere,
                vmem,
                vmem,
                vmem,
                anywhere,
                vmem,
                vmem,
            ],
            out_specs=(vmem, vmem),
            scratch_shapes=[
                pltpu.VMEM((HEADS, ROWS, 2 * HD), BF16),
                pltpu.VMEM((HEADS, ROWS, 2 * HD), BF16),
                pltpu.VMEM((8, HD), F32),
                pltpu.VMEM((seq, 2 * HD), BF16),
                pltpu.VMEM((seq, 2 * HD), BF16),
                pltpu.VMEM((seq, 2 * HD), BF16),
                pltpu.VMEM((n_ctx, 8, HD), F32),
                pltpu.VMEM((seq, HD), F32),
                pltpu.VMEM((tile, seq), F32),
                pltpu.VMEM((tile, seq), BF16),
                pltpu.VMEM((tile, seq), BF16),
                pltpu.VMEM((n_ctx // 2, tile, HD), BF16),
                pltpu.VMEM((ROWS, HEADS * HD), BF16),
                pltpu.VMEM((HEADS * HD, width), BF16),
                pltpu.VMEM((8, width // 8), F32),
                pltpu.VMEM((n_ctx, 8, width // 8), F32),
                pltpu.VMEM((8, width // 8), F32),
                pltpu.VMEM((n_dp, 8, width // 8), F32),
                dma,
                dma((HEADS,)),
                dma((HEADS,)),
                dma((HEADS,)),
                dma((HEADS,)),
                dma((HEADS,)),
                dma,
                dma,
                dma((n_ctx,)),
                dma,
                dma((n_ctx,)),
                dma,
                dma((n_ctx,)),
                dma,
                dma((n_dp,)),
                dma,
            ],
            compiler_params=pltpu.CompilerParams(
                collective_id=0,
                has_side_effects=True,
                vmem_limit_bytes=48 * 1024 * 1024,
            ),
        )(
            block_order,
            queries,
            keys,
            values,
            tangent_queries,
            tangent_keys,
            tangent_values,
            clip_ids,
            jnp.asarray(inside),
            jnp.asarray(start),
            out_weight,
            layer_scale.reshape(1, width),
            cotangent,
        )
        return branch, grad.reshape(width)

    tokens = P("dp", "ctx", None)
    in_specs = (tokens,) * 6 + (P("dp", "ctx"), P(), P(), P(), tokens)
    return jax.shard_map(
        local, mesh=mesh, in_specs=in_specs, out_specs=(tokens, P()), check_vma=False
    )
```

```python
import math

import jax
import jax.numpy as jnp
import numpy as np
from jax import lax
from jax.experimental import pallas as pl
from jax.experimental.pallas import tpu as pltpu
from jax.sharding import PartitionSpec as P

MESH = pl.DeviceIdType.MESH
HEADS = 12
HD = 128
ROWS = 128
F32 = jnp.float32
BF16 = jnp.bfloat16


def owner_of(head):
    row, rest = head // 6, head % 6
    return 8 * row + rest + (rest + 2 * row) // 3


def kernel(
    n_ctx,
    n_dp,
    order_hbm,
    q_hbm,
    k_hbm,
    v_ref,
    tq_hbm,
    tk_hbm,
    tv_ref,
    ids_hbm,
    turn_hbm,
    w_hbm,
    ls_hbm,
    cot_hbm,
    branch_ref,
    grad_ref,
    order_ref,
    q_ref,
    k_ref,
    tq_ref,
    tk_ref,
    ids_ref,
    turn_ref,
    ls_ref,
    cot_ref,
    kk_stage,
    qq_stage,
    id_stage,
    kk,
    vv,
    qq,
    id_rows,
    id_cols,
    s_buf,
    wb_buf,
    tb_buf,
    out_stage,
    attn,
    w_buf,
    g_part,
    g_ctx,
    g_sum,
    g_dp,
    load_sem,
    send_k,
    send_v,
    send_tv,
    send_q,
    send_id,
    recv_k,
    recv_v,
    recv_q,
    recv_id,
    send_out,
    recv_out,
    send_gc,
    recv_gc,
    send_gd,
    recv_gd,
):
    me = lax.axis_index("ctx")
    me_dp = lax.axis_index("dp")
    chip, core = me // 2, me % 2
    row, col = chip // 4, chip % 4
    my_head = 6 * row + (3 * col + 1 - row) // 2 + core
    is_owner = core * ((row + col) % 2) == 0
    chips = n_ctx // 2

    barrier = pltpu.get_barrier_semaphore()

    @pl.loop(1, n_ctx)
    def _(i):
        pl.semaphore_signal(
            barrier, inc=1, device_id={"ctx": (me + i) % n_ctx}, device_id_type=MESH
        )

    @pl.loop(1, n_dp)
    def _(i):
        pl.semaphore_signal(
            barrier, inc=1, device_id={"dp": (me_dp + i) % n_dp}, device_id_type=MESH
        )

    loads = [
        pltpu.make_async_copy(src, dst, load_sem.at[i])
        for i, (src, dst) in enumerate(
            [
                (order_hbm, order_ref),
                (turn_hbm, turn_ref),
                (k_hbm, k_ref),
                (tk_hbm, tk_ref),
                (q_hbm, q_ref),
                (tq_hbm, tq_ref),
                (ids_hbm, ids_ref),
                (ls_hbm, ls_ref),
                (cot_hbm, cot_ref),
                (w_hbm, w_buf),
            ]
        )
    ]
    for load in loads:
        load.start()

    for load in loads[:4]:
        load.wait()
    place = order_ref[me]
    cos_b = turn_ref[0, pl.ds(ROWS + place, 1), :]
    sin_b = turn_ref[1, pl.ds(ROWS + place, 1), :]
    cos_t, sin_t = turn_ref[0, 0:ROWS, :], turn_ref[1, 0:ROWS, :]
    lane = lax.broadcasted_iota(jnp.int32, (ROWS, HD), 1)
    cosine = cos_b * cos_t - sin_b * sin_t
    sine = sin_b * cos_t + cos_b * sin_t
    sine = jnp.where(lane < HD // 2, -sine, sine)

    def turned(x, c, s):
        x = x.astype(F32)
        return (x * c + pltpu.roll(x, HD // 2, axis=1) * s).astype(BF16)

    for h in range(HEADS):
        cols = slice(h * HD, (h + 1) * HD)
        kk_stage[h, :, 0:HD] = turned(k_ref[0, :, cols], cosine, sine)
        kk_stage[h, :, HD : 2 * HD] = turned(tk_ref[0, :, cols], cosine, sine)
    for load in loads[4:7]:
        load.wait()
    cosine, sine = cosine * 0.0625, sine * 0.0625
    for h in range(HEADS):
        cols = slice(h * HD, (h + 1) * HD)
        qq_stage[h, :, 0:HD] = turned(tq_ref[0, :, cols], cosine, sine)
        qq_stage[h, :, HD : 2 * HD] = turned(q_ref[0, :, cols], cosine, sine)
    id_stage[...] = jnp.broadcast_to(ids_ref[...].astype(F32), (8, HD))

    pl.semaphore_wait(barrier, n_ctx - 1 + n_dp - 1)

    rows_here = pl.ds(pl.multiple_of(me * ROWS, ROWS), ROWS)

    def pieces(h):
        cols = pl.ds(pl.multiple_of(h * HD, HD), HD)
        return [
            (id_stage, id_rows.at[me], send_id.at[h], recv_id),
            (kk_stage.at[h], kk.at[rows_here, :], send_k.at[h], recv_k),
            (v_ref.at[0, :, cols], vv.at[rows_here, pl.ds(0, HD)], send_v.at[h], recv_v),
            (tv_ref.at[0, :, cols], vv.at[rows_here, pl.ds(HD, HD)], send_tv.at[h], recv_v),
            (qq_stage.at[h], qq.at[rows_here, :], send_q.at[h], recv_q.at[me]),
        ]

    def remote(piece, to):
        src, dst, ssem, rsem = piece
        return pltpu.make_async_remote_copy(
            src_ref=src,
            dst_ref=dst,
            send_sem=ssem,
            recv_sem=rsem,
            device_id={"ctx": to},
            device_id_type=MESH,
        )

    def start_sends(which):
        @pl.loop(0, HEADS)
        def _(i):
            h = (i + my_head) % HEADS
            to = owner_of(h)

            @pl.when(to != me)
            def _():
                for p in which:
                    remote(pieces(h)[p], to).start()

            @pl.when(to == me)
            def _():
                for p in which:
                    src, dst, _, rsem = pieces(h)[p]
                    pltpu.make_async_copy(src, dst, rsem).start()

    start_sends((0, 1, 2, 3))
    start_sends((4,))

    @pl.when(is_owner)
    def _():
        pltpu.make_async_copy(id_rows, id_rows, recv_id).wait()

        @pl.loop(0, n_ctx)
        def _(j):
            ids = jnp.broadcast_to(id_rows[j, 0:1, :], (ROWS, HD))
            id_cols[pl.ds(pl.multiple_of(j * ROWS, ROWS), ROWS), :] = ids.T

        pltpu.make_async_copy(kk, kk, recv_k).wait()
        pltpu.make_async_copy(vv, vv, recv_v).wait()

        tile = 2 * ROWS
        step = math.log2(math.e) * math.sqrt(2.0)
        contract_last = (((1,), (1,)), ((), ()))

        @pl.loop(0, chips)
        def _(t):
            at = (chip + chips - t) % chips
            rows = pl.ds(pl.multiple_of(at * tile, tile), tile)
            for c in range(2):
                block = at * 2 + c
                part = qq.at[pl.ds(pl.multiple_of(block * ROWS, ROWS), ROWS), :]
                pltpu.make_async_copy(part, part, recv_q.at[block]).wait()
            both = qq[rows, :]
            q = both[:, HD : 2 * HD]
            mine = id_cols[rows, :]
            best = jnp.full((tile, HD), -jnp.inf, F32)
            for c in range(chips):
                keys = kk[c * tile : (c + 1) * tile, 0:HD]
                s = lax.dot_general(q, keys, contract_last, preferred_element_type=F32)
                for half in range(2):
                    j = 2 * c + half
                    theirs = jnp.broadcast_to(id_rows[j, 0:1, :], (tile, HD))
                    s_half = jnp.where(mine == theirs, s[:, half * HD : (half + 1) * HD], -jnp.inf)
                    s_buf[:, j * HD : (j + 1) * HD] = s_half
                    best = jnp.maximum(best, s_half)
            best = jnp.broadcast_to(jnp.max(best, axis=1, keepdims=True), (tile, HD))
            total = jnp.zeros((tile, HD), F32)
            weighted = jnp.zeros((tile, HD), F32)
            for c in range(chips):
                keys = kk[c * tile : (c + 1) * tile, :]
                slopes = lax.dot_general(both, keys, contract_last, preferred_element_type=F32)
                for half in range(2):
                    j = 2 * c + half
                    there = slice(j * HD, (j + 1) * HD)
                    w = jnp.exp2((s_buf[:, there] - best) * step)
                    tilted = w * slopes[:, half * HD : (half + 1) * HD]
                    total = total + w
                    weighted = weighted + tilted
                    wb_buf[:, there] = w.astype(BF16)
                    tb_buf[:, there] = tilted.astype(BF16)
            sums = jnp.dot(wb_buf[...], vv[...], preferred_element_type=F32)
            slope_part = jnp.dot(tb_buf[...], vv[:, 0:HD], preferred_element_type=F32)
            total = jnp.sum(total, axis=1, keepdims=True)
            weighted = jnp.sum(weighted, axis=1, keepdims=True) * math.sqrt(2.0)
            primal, spread = sums[:, 0:HD], sums[:, HD : 2 * HD]
            result = (slope_part * math.sqrt(2.0) + spread) / total - (weighted / total) * (
                primal / total
            )
            out_stage[at] = result.astype(BF16)
            for c in range(2):
                block = at * 2 + c
                src = out_stage.at[at, pl.ds(c * ROWS, ROWS), :]
                dst = attn.at[:, pl.ds(pl.multiple_of(my_head * HD, HD), HD)]

                @pl.when(block != me)
                def _():
                    remote((src, dst, send_out.at[block], recv_out), block).start()

                @pl.when(block == me)
                def _():
                    pltpu.make_async_copy(src, dst, recv_out).start()

    for load in loads[7:]:
        load.wait()
    pltpu.make_async_copy(attn, attn, recv_out).wait()

    width = w_buf.shape[1]
    wide = width // 8
    for n in range(8):
        cols = slice(n * wide, (n + 1) * wide)
        projected = jnp.dot(attn[...], w_buf[:, cols], preferred_element_type=F32)
        branch_ref[0, :, cols] = (ls_ref[:, cols] * projected).astype(BF16)
        weighed = cot_ref[0, :, cols].astype(F32) * projected
        g_part[n : n + 1, :] = jnp.sum(weighed, axis=0, keepdims=True)

    def exchange(axis, index, size, src, dst, ssem, rsem):
        def copy_to(i):
            return pltpu.make_async_remote_copy(
                src_ref=src,
                dst_ref=dst.at[index],
                send_sem=ssem.at[i],
                recv_sem=rsem,
                device_id={axis: (index + i) % size},
                device_id_type=MESH,
            )

        @pl.loop(1, size)
        def _(i):
            copy_to(i).start()

        pltpu.make_async_copy(src, dst.at[index], rsem).start()
        pltpu.make_async_copy(dst, dst, rsem).wait()
        return copy_to

    copy_c = exchange("ctx", me, n_ctx, g_part, g_ctx, send_gc, recv_gc)
    acc = g_ctx[0]
    for i in range(1, n_ctx):
        acc = acc + g_ctx[i]
    g_sum[...] = acc
    copy_d = exchange("dp", me_dp, n_dp, g_sum, g_dp, send_gd, recv_gd)
    acc = g_dp[0]
    for i in range(1, n_dp):
        acc = acc + g_dp[i]
    acc = acc / math.sqrt(n_ctx * n_dp * ROWS)
    for n in range(8):
        for c in range(wide // HD):
            at = n * (wide // HD) + c
            grad_ref[at : at + 1, :] = acc[n : n + 1, c * HD : (c + 1) * HD]

    @pl.loop(0, HEADS)
    def _(h):
        to = owner_of(h)

        @pl.when(to != me)
        def _():
            for piece in pieces(h):
                remote(piece, to).wait_send()

    @pl.when(is_owner)
    def _():
        @pl.loop(0, n_ctx)
        def _(block):
            @pl.when(block != me)
            def _():
                src = out_stage.at[block // 2, pl.ds((block % 2) * ROWS, ROWS), :]
                dst = attn.at[:, pl.ds(pl.multiple_of(my_head * HD, HD), HD)]
                remote((src, dst, send_out.at[block], recv_out), block).wait_send()

    @pl.loop(1, n_ctx)
    def _(i):
        copy_c(i).wait_send()

    @pl.loop(1, n_dp)
    def _(i):
        copy_d(i).wait_send()


def turn_tables(blocks):
    frequency = 10000.0 ** (-np.arange(HD // 2, dtype=np.float64) / (HD // 2))
    frequency = np.concatenate([frequency, frequency])
    inside = np.arange(ROWS, dtype=np.float64)[:, None] * frequency
    start = ROWS * np.arange(blocks, dtype=np.float64)[:, None] * frequency
    angles = np.concatenate([inside, start])
    return np.stack([np.cos(angles), np.sin(angles)]).astype(np.float32)


def solution(mesh):
    n_ctx, n_dp = mesh.shape["ctx"], mesh.shape["dp"]
    turns = turn_tables(n_ctx)

    def local(
        queries,
        keys,
        values,
        tangent_queries,
        tangent_keys,
        tangent_values,
        clip_ids,
        block_order,
        out_weight,
        layer_scale,
        cotangent,
    ):
        width = out_weight.shape[1]
        seq = n_ctx * ROWS
        tile = 2 * ROWS
        vmem = pl.BlockSpec(memory_space=pltpu.VMEM)
        dma = pltpu.SemaphoreType.DMA
        branch, grad = pl.pallas_call(
            lambda *refs: kernel(n_ctx, n_dp, *refs),
            out_shape=(
                jax.ShapeDtypeStruct((1, ROWS, width), BF16),
                jax.ShapeDtypeStruct((width // HD, HD), F32),
            ),
            in_specs=[pl.BlockSpec(memory_space=pltpu.HBM)] * 12,
            out_specs=(vmem, vmem),
            scratch_shapes=[
                pltpu.SMEM((n_ctx,), jnp.int32),
                pltpu.VMEM((1, ROWS, HEADS * HD), BF16),
                pltpu.VMEM((1, ROWS, HEADS * HD), BF16),
                pltpu.VMEM((1, ROWS, HEADS * HD), BF16),
                pltpu.VMEM((1, ROWS, HEADS * HD), BF16),
                pltpu.VMEM((1, ROWS), jnp.int32),
                pltpu.VMEM((2, ROWS + n_ctx, HD), F32),
                pltpu.VMEM((1, width), F32),
                pltpu.VMEM((1, ROWS, width), BF16),
                pltpu.VMEM((HEADS, ROWS, 2 * HD), BF16),
                pltpu.VMEM((HEADS, ROWS, 2 * HD), BF16),
                pltpu.VMEM((8, HD), F32),
                pltpu.VMEM((seq, 2 * HD), BF16),
                pltpu.VMEM((seq, 2 * HD), BF16),
                pltpu.VMEM((seq, 2 * HD), BF16),
                pltpu.VMEM((n_ctx, 8, HD), F32),
                pltpu.VMEM((seq, HD), F32),
                pltpu.VMEM((tile, seq), F32),
                pltpu.VMEM((tile, seq), BF16),
                pltpu.VMEM((tile, seq), BF16),
                pltpu.VMEM((n_ctx // 2, tile, HD), BF16),
                pltpu.VMEM((ROWS, HEADS * HD), BF16),
                pltpu.VMEM((HEADS * HD, width), BF16),
                pltpu.VMEM((8, width // 8), F32),
                pltpu.VMEM((n_ctx, 8, width // 8), F32),
                pltpu.VMEM((8, width // 8), F32),
                pltpu.VMEM((n_dp, 8, width // 8), F32),
                dma((10,)),
                dma((HEADS,)),
                dma((HEADS,)),
                dma((HEADS,)),
                dma((HEADS,)),
                dma((HEADS,)),
                dma,
                dma,
                dma((n_ctx,)),
                dma,
                dma((n_ctx,)),
                dma,
                dma((n_ctx,)),
                dma,
                dma((n_dp,)),
                dma,
            ],
            compiler_params=pltpu.CompilerParams(
                collective_id=0,
                has_side_effects=True,
                vmem_limit_bytes=48 * 1024 * 1024,
            ),
        )(
            *[pltpu.with_memory_space_constraint(x, pltpu.HBM) for x in (
                block_order,
                queries,
                keys,
                values,
                tangent_queries,
                tangent_keys,
                tangent_values,
                clip_ids,
                jnp.asarray(turns),
                out_weight,
                layer_scale.reshape(1, width),
                cotangent,
            )]
        )
        return branch, grad.reshape(width)

    tokens = P("dp", "ctx", None)
    in_specs = (tokens,) * 6 + (P("dp", "ctx"), P(), P(), P(), tokens)
    return jax.shard_map(
        local, mesh=mesh, in_specs=in_specs, out_specs=(tokens, P()), check_vma=False
    )
```

```python
import math

import jax
import jax.numpy as jnp
import numpy as np
from jax import lax
from jax.experimental import pallas as pl
from jax.experimental.pallas import tpu as pltpu
from jax.sharding import PartitionSpec as P

MESH = pl.DeviceIdType.MESH
HEADS = 12
HD = 128
ROWS = 128
F32 = jnp.float32
BF16 = jnp.bfloat16


def owner_of(head):
    row, rest = head // 6, head % 6
    return 8 * row + rest + (rest + 2 * row) // 3


def kernel(
    n_ctx,
    n_dp,
    order_hbm,
    q_hbm,
    k_hbm,
    v_ref,
    tq_hbm,
    tk_hbm,
    tv_ref,
    ids_hbm,
    turn_hbm,
    w_hbm,
    ls_hbm,
    cot_hbm,
    branch_ref,
    grad_ref,
    order_ref,
    q_ref,
    k_ref,
    tq_ref,
    tk_ref,
    ids_ref,
    turn_ref,
    ls_ref,
    cot_ref,
    kk_stage,
    qq_stage,
    id_stage,
    kk,
    vv,
    qq,
    id_rows,
    id_cols,
    s_buf,
    wb_buf,
    tb_buf,
    out_stage,
    attn,
    w_buf,
    g_part,
    g_ctx,
    g_sum,
    g_dp,
    load_sem,
    send_k,
    send_v,
    send_tv,
    send_q,
    send_id,
    recv_k,
    recv_v,
    recv_q,
    recv_id,
    send_out,
    recv_out,
    send_gc,
    recv_gc,
    send_gd,
    recv_gd,
):
    me = lax.axis_index("ctx")
    me_dp = lax.axis_index("dp")
    chip, core = me // 2, me % 2
    row, col = chip // 4, chip % 4
    my_head = 6 * row + (3 * col + 1 - row) // 2 + core
    is_owner = core * ((row + col) % 2) == 0
    chips = n_ctx // 2

    barrier = pltpu.get_barrier_semaphore()

    @pl.loop(1, n_ctx)
    def _(i):
        pl.semaphore_signal(
            barrier, inc=1, device_id={"ctx": (me + i) % n_ctx}, device_id_type=MESH
        )

    @pl.loop(1, n_dp)
    def _(i):
        pl.semaphore_signal(
            barrier, inc=1, device_id={"dp": (me_dp + i) % n_dp}, device_id_type=MESH
        )

    loads = [
        pltpu.make_async_copy(src, dst, load_sem.at[i])
        for i, (src, dst) in enumerate(
            [
                (order_hbm, order_ref),
                (turn_hbm, turn_ref),
                (k_hbm, k_ref),
                (tk_hbm, tk_ref),
                (q_hbm, q_ref),
                (tq_hbm, tq_ref),
                (ids_hbm, ids_ref),
                (ls_hbm, ls_ref),
                (cot_hbm, cot_ref),
                (w_hbm, w_buf),
            ]
        )
    ]
    for load in loads:
        load.start()

    for load in loads[:4]:
        load.wait()
    place = order_ref[me]
    cos_b = turn_ref[0, pl.ds(ROWS + place, 1), :]
    sin_b = turn_ref[1, pl.ds(ROWS + place, 1), :]
    cos_t, sin_t = turn_ref[0, 0:ROWS, :], turn_ref[1, 0:ROWS, :]
    lane = lax.broadcasted_iota(jnp.int32, (ROWS, HD), 1)
    cosine = cos_b * cos_t - sin_b * sin_t
    sine = sin_b * cos_t + cos_b * sin_t
    sine = jnp.where(lane < HD // 2, -sine, sine)

    def turned(x, c, s):
        x = x.astype(F32)
        return (x * c + pltpu.roll(x, HD // 2, axis=1) * s).astype(BF16)

    for h in range(HEADS):
        cols = slice(h * HD, (h + 1) * HD)
        kk_stage[h, :, 0:HD] = turned(k_ref[0, :, cols], cosine, sine)
        kk_stage[h, :, HD : 2 * HD] = turned(tk_ref[0, :, cols], cosine, sine)
    for load in loads[4:7]:
        load.wait()
    cosine, sine = cosine * 0.0625, sine * 0.0625
    for h in range(HEADS):
        cols = slice(h * HD, (h + 1) * HD)
        qq_stage[h, :, 0:HD] = turned(tq_ref[0, :, cols], cosine, sine)
        qq_stage[h, :, HD : 2 * HD] = turned(q_ref[0, :, cols], cosine, sine)
    id_stage[...] = jnp.broadcast_to(ids_ref[...].astype(F32), (8, HD))

    pl.semaphore_wait(barrier, n_ctx - 1 + n_dp - 1)

    rows_here = pl.ds(pl.multiple_of(me * ROWS, ROWS), ROWS)

    def pieces(h):
        cols = pl.ds(pl.multiple_of(h * HD, HD), HD)
        return [
            (id_stage, id_rows.at[me], send_id.at[h], recv_id),
            (kk_stage.at[h], kk.at[rows_here, :], send_k.at[h], recv_k),
            (v_ref.at[0, :, cols], vv.at[rows_here, pl.ds(0, HD)], send_v.at[h], recv_v),
            (tv_ref.at[0, :, cols], vv.at[rows_here, pl.ds(HD, HD)], send_tv.at[h], recv_v),
            (qq_stage.at[h], qq.at[rows_here, :], send_q.at[h], recv_q.at[me]),
        ]

    def remote(piece, to):
        src, dst, ssem, rsem = piece
        return pltpu.make_async_remote_copy(
            src_ref=src,
            dst_ref=dst,
            send_sem=ssem,
            recv_sem=rsem,
            device_id={"ctx": to},
            device_id_type=MESH,
        )

    def start_sends(which):
        @pl.loop(0, HEADS)
        def _(i):
            h = (i + my_head) % HEADS
            to = owner_of(h)

            @pl.when(to != me)
            def _():
                for p in which:
                    remote(pieces(h)[p], to).start()

            @pl.when(to == me)
            def _():
                for p in which:
                    src, dst, _, rsem = pieces(h)[p]
                    pltpu.make_async_copy(src, dst, rsem).start()

    start_sends((0, 1, 2, 3))
    start_sends((4,))

    @pl.when(is_owner)
    def _():
        pltpu.make_async_copy(id_rows, id_rows, recv_id).wait()

        @pl.loop(0, n_ctx)
        def _(j):
            ids = jnp.broadcast_to(id_rows[j, 0:1, :], (ROWS, HD))
            id_cols[pl.ds(pl.multiple_of(j * ROWS, ROWS), ROWS), :] = ids.T

        pltpu.make_async_copy(kk, kk, recv_k).wait()
        pltpu.make_async_copy(vv, vv, recv_v).wait()

        tile = 2 * ROWS
        step = math.log2(math.e) * math.sqrt(2.0)
        contract_last = (((1,), (1,)), ((), ()))

        @pl.loop(0, chips)
        def _(t):
            at = (chip + 2 * chips - 1 - t) % chips
            rows = pl.ds(pl.multiple_of(at * tile, tile), tile)
            for c in range(2):
                block = at * 2 + c
                part = qq.at[pl.ds(pl.multiple_of(block * ROWS, ROWS), ROWS), :]
                pltpu.make_async_copy(part, part, recv_q.at[block]).wait()
            both = qq[rows, :]
            q = both[:, HD : 2 * HD]
            mine = id_cols[rows, :]
            best = jnp.full((tile, HD), -jnp.inf, F32)
            for c in range(chips):
                keys = kk[c * tile : (c + 1) * tile, 0:HD]
                s = lax.dot_general(q, keys, contract_last, preferred_element_type=F32)
                for half in range(2):
                    j = 2 * c + half
                    theirs = jnp.broadcast_to(id_rows[j, 0:1, :], (tile, HD))
                    s_half = jnp.where(mine == theirs, s[:, half * HD : (half + 1) * HD], -jnp.inf)
                    s_buf[:, j * HD : (j + 1) * HD] = s_half
                    best = jnp.maximum(best, s_half)
            best = jnp.broadcast_to(jnp.max(best, axis=1, keepdims=True), (tile, HD))
            total = jnp.zeros((tile, HD), F32)
            weighted = jnp.zeros((tile, HD), F32)
            for c in range(chips):
                keys = kk[c * tile : (c + 1) * tile, :]
                slopes = lax.dot_general(both, keys, contract_last, preferred_element_type=F32)
                for half in range(2):
                    j = 2 * c + half
                    there = slice(j * HD, (j + 1) * HD)
                    w = jnp.exp2((s_buf[:, there] - best) * step)
                    tilted = w * slopes[:, half * HD : (half + 1) * HD]
                    total = total + w
                    weighted = weighted + tilted
                    wb_buf[:, there] = w.astype(BF16)
                    tb_buf[:, there] = tilted.astype(BF16)
            sums = jnp.dot(wb_buf[...], vv[...], preferred_element_type=F32)
            slope_part = jnp.dot(tb_buf[...], vv[:, 0:HD], preferred_element_type=F32)
            total = jnp.sum(total, axis=1, keepdims=True)
            weighted = jnp.sum(weighted, axis=1, keepdims=True) * math.sqrt(2.0)
            primal, spread = sums[:, 0:HD], sums[:, HD : 2 * HD]
            result = (slope_part * math.sqrt(2.0) + spread) / total - (weighted / total) * (
                primal / total
            )
            out_stage[at] = result.astype(BF16)
            for c in range(2):
                block = at * 2 + c
                src = out_stage.at[at, pl.ds(c * ROWS, ROWS), :]
                dst = attn.at[:, pl.ds(pl.multiple_of(my_head * HD, HD), HD)]

                @pl.when(block != me)
                def _():
                    remote((src, dst, send_out.at[block], recv_out), block).start()

                @pl.when(block == me)
                def _():
                    pltpu.make_async_copy(src, dst, recv_out).start()

    for load in loads[7:]:
        load.wait()
    pltpu.make_async_copy(attn, attn, recv_out).wait()

    width = w_buf.shape[1]
    wide = width // 8
    for n in range(8):
        cols = slice(n * wide, (n + 1) * wide)
        projected = jnp.dot(attn[...], w_buf[:, cols], preferred_element_type=F32)
        branch_ref[0, :, cols] = (ls_ref[:, cols] * projected).astype(BF16)
        weighed = cot_ref[0, :, cols].astype(F32) * projected
        g_part[n : n + 1, :] = jnp.sum(weighed, axis=0, keepdims=True).astype(BF16)

    def exchange(axis, index, size, src, dst, ssem, rsem):
        def copy_to(i):
            return pltpu.make_async_remote_copy(
                src_ref=src,
                dst_ref=dst.at[index],
                send_sem=ssem.at[i],
                recv_sem=rsem,
                device_id={axis: (index + i) % size},
                device_id_type=MESH,
            )

        @pl.loop(1, size)
        def _(i):
            copy_to(i).start()

        pltpu.make_async_copy(src, dst.at[index], rsem).start()
        pltpu.make_async_copy(dst, dst, rsem).wait()
        return copy_to

    copy_c = exchange("ctx", me, n_ctx, g_part, g_ctx, send_gc, recv_gc)
    acc = g_ctx[0].astype(F32)
    for i in range(1, n_ctx):
        acc = acc + g_ctx[i].astype(F32)
    g_sum[...] = acc.astype(BF16)
    copy_d = exchange("dp", me_dp, n_dp, g_sum, g_dp, send_gd, recv_gd)
    acc = g_dp[0].astype(F32)
    for i in range(1, n_dp):
        acc = acc + g_dp[i].astype(F32)
    acc = acc / math.sqrt(n_ctx * n_dp * ROWS)
    for n in range(8):
        for c in range(wide // HD):
            at = n * (wide // HD) + c
            grad_ref[at : at + 1, :] = acc[n : n + 1, c * HD : (c + 1) * HD]

    @pl.loop(0, HEADS)
    def _(h):
        to = owner_of(h)

        @pl.when(to != me)
        def _():
            for piece in pieces(h):
                remote(piece, to).wait_send()

    @pl.when(is_owner)
    def _():
        @pl.loop(0, n_ctx)
        def _(block):
            @pl.when(block != me)
            def _():
                src = out_stage.at[block // 2, pl.ds((block % 2) * ROWS, ROWS), :]
                dst = attn.at[:, pl.ds(pl.multiple_of(my_head * HD, HD), HD)]
                remote((src, dst, send_out.at[block], recv_out), block).wait_send()

    @pl.loop(1, n_ctx)
    def _(i):
        copy_c(i).wait_send()

    @pl.loop(1, n_dp)
    def _(i):
        copy_d(i).wait_send()


def turn_tables(blocks):
    frequency = 10000.0 ** (-np.arange(HD // 2, dtype=np.float64) / (HD // 2))
    frequency = np.concatenate([frequency, frequency])
    inside = np.arange(ROWS, dtype=np.float64)[:, None] * frequency
    start = ROWS * np.arange(blocks, dtype=np.float64)[:, None] * frequency
    angles = np.concatenate([inside, start])
    return np.stack([np.cos(angles), np.sin(angles)]).astype(np.float32)


def solution(mesh):
    n_ctx, n_dp = mesh.shape["ctx"], mesh.shape["dp"]
    turns = turn_tables(n_ctx)

    def local(
        queries,
        keys,
        values,
        tangent_queries,
        tangent_keys,
        tangent_values,
        clip_ids,
        block_order,
        out_weight,
        layer_scale,
        cotangent,
    ):
        width = out_weight.shape[1]
        seq = n_ctx * ROWS
        tile = 2 * ROWS
        vmem = pl.BlockSpec(memory_space=pltpu.VMEM)
        dma = pltpu.SemaphoreType.DMA
        branch, grad = pl.pallas_call(
            lambda *refs: kernel(n_ctx, n_dp, *refs),
            out_shape=(
                jax.ShapeDtypeStruct((1, ROWS, width), BF16),
                jax.ShapeDtypeStruct((width // HD, HD), F32),
            ),
            in_specs=[pl.BlockSpec(memory_space=pltpu.HBM)] * 12,
            out_specs=(vmem, vmem),
            scratch_shapes=[
                pltpu.SMEM((n_ctx,), jnp.int32),
                pltpu.VMEM((1, ROWS, HEADS * HD), BF16),
                pltpu.VMEM((1, ROWS, HEADS * HD), BF16),
                pltpu.VMEM((1, ROWS, HEADS * HD), BF16),
                pltpu.VMEM((1, ROWS, HEADS * HD), BF16),
                pltpu.VMEM((1, ROWS), jnp.int32),
                pltpu.VMEM((2, ROWS + n_ctx, HD), F32),
                pltpu.VMEM((1, width), F32),
                pltpu.VMEM((1, ROWS, width), BF16),
                pltpu.VMEM((HEADS, ROWS, 2 * HD), BF16),
                pltpu.VMEM((HEADS, ROWS, 2 * HD), BF16),
                pltpu.VMEM((8, HD), F32),
                pltpu.VMEM((seq, 2 * HD), BF16),
                pltpu.VMEM((seq, 2 * HD), BF16),
                pltpu.VMEM((seq, 2 * HD), BF16),
                pltpu.VMEM((n_ctx, 8, HD), F32),
                pltpu.VMEM((seq, HD), F32),
                pltpu.VMEM((tile, seq), F32),
                pltpu.VMEM((tile, seq), BF16),
                pltpu.VMEM((tile, seq), BF16),
                pltpu.VMEM((n_ctx // 2, tile, HD), BF16),
                pltpu.VMEM((ROWS, HEADS * HD), BF16),
                pltpu.VMEM((HEADS * HD, width), BF16),
                pltpu.VMEM((8, width // 8), BF16),
                pltpu.VMEM((n_ctx, 8, width // 8), BF16),
                pltpu.VMEM((8, width // 8), BF16),
                pltpu.VMEM((n_dp, 8, width // 8), BF16),
                dma((10,)),
                dma((HEADS,)),
                dma((HEADS,)),
                dma((HEADS,)),
                dma((HEADS,)),
                dma((HEADS,)),
                dma,
                dma,
                dma((n_ctx,)),
                dma,
                dma((n_ctx,)),
                dma,
                dma((n_ctx,)),
                dma,
                dma((n_dp,)),
                dma,
            ],
            compiler_params=pltpu.CompilerParams(
                collective_id=0,
                has_side_effects=True,
                vmem_limit_bytes=48 * 1024 * 1024,
            ),
        )(
            *[pltpu.with_memory_space_constraint(x, pltpu.HBM) for x in (
                block_order,
                queries,
                keys,
                values,
                tangent_queries,
                tangent_keys,
                tangent_values,
                clip_ids,
                jnp.asarray(turns),
                out_weight,
                layer_scale.reshape(1, width),
                cotangent,
            )]
        )
        return branch, grad.reshape(width)

    tokens = P("dp", "ctx", None)
    in_specs = (tokens,) * 6 + (P("dp", "ctx"), P(), P(), P(), tokens)
    return jax.shard_map(
        local, mesh=mesh, in_specs=in_specs, out_specs=(tokens, P()), check_vma=False
    )
```

```python
import math

import jax
import jax.numpy as jnp
import numpy as np
from jax import lax
from jax.experimental import pallas as pl
from jax.experimental.pallas import tpu as pltpu
from jax.sharding import PartitionSpec as P

MESH = pl.DeviceIdType.MESH
HEADS = 12
HD = 128
ROWS = 128
F32 = jnp.float32
BF16 = jnp.bfloat16


def owner_of(head):
    row, rest = head // 6, head % 6
    return 8 * row + rest + (rest + 2 * row) // 3


def kernel(
    n_ctx,
    n_dp,
    order_hbm,
    q_hbm,
    k_hbm,
    v_ref,
    tq_hbm,
    tk_hbm,
    tv_ref,
    ids_hbm,
    turn_hbm,
    w_hbm,
    ls_hbm,
    cot_hbm,
    branch_ref,
    grad_ref,
    order_ref,
    q_ref,
    k_ref,
    tq_ref,
    tk_ref,
    ids_ref,
    turn_ref,
    ls_ref,
    cot_ref,
    kk_stage,
    qq_stage,
    id_stage,
    kk,
    vv,
    qq,
    id_rows,
    id_cols,
    s_buf,
    wb_buf,
    tb_buf,
    v_ones,
    out_stage,
    attn,
    w_buf,
    g_part,
    g_ctx,
    g_sum,
    g_dp,
    load_sem,
    send_k,
    send_v,
    send_tv,
    send_q,
    send_id,
    recv_k,
    recv_v,
    recv_q,
    recv_id,
    send_out,
    recv_out,
    send_gc,
    recv_gc,
    send_gd,
    recv_gd,
):
    me = lax.axis_index("ctx")
    me_dp = lax.axis_index("dp")
    chip, core = me // 2, me % 2
    row, col = chip // 4, chip % 4
    my_head = 6 * row + (3 * col + 1 - row) // 2 + core
    is_owner = core * ((row + col) % 2) == 0
    chips = n_ctx // 2

    barrier = pltpu.get_barrier_semaphore()

    @pl.loop(1, n_ctx)
    def _(i):
        pl.semaphore_signal(
            barrier, inc=1, device_id={"ctx": (me + i) % n_ctx}, device_id_type=MESH
        )

    @pl.loop(1, n_dp)
    def _(i):
        pl.semaphore_signal(
            barrier, inc=1, device_id={"dp": (me_dp + i) % n_dp}, device_id_type=MESH
        )

    loads = [
        pltpu.make_async_copy(src, dst, load_sem.at[i])
        for i, (src, dst) in enumerate(
            [
                (order_hbm, order_ref),
                (turn_hbm, turn_ref),
                (k_hbm, k_ref),
                (tk_hbm, tk_ref),
                (q_hbm, q_ref),
                (tq_hbm, tq_ref),
                (ids_hbm, ids_ref),
                (ls_hbm, ls_ref),
                (cot_hbm, cot_ref),
                (w_hbm, w_buf),
            ]
        )
    ]
    for load in loads:
        load.start()

    for load in loads[:4]:
        load.wait()
    place = order_ref[me]
    cos_b = turn_ref[0, pl.ds(ROWS + place, 1), :]
    sin_b = turn_ref[1, pl.ds(ROWS + place, 1), :]
    cos_t, sin_t = turn_ref[0, 0:ROWS, :], turn_ref[1, 0:ROWS, :]
    lane = lax.broadcasted_iota(jnp.int32, (ROWS, HD), 1)
    cosine = cos_b * cos_t - sin_b * sin_t
    sine = sin_b * cos_t + cos_b * sin_t
    sine = jnp.where(lane < HD // 2, -sine, sine)

    def turned(x, c, s):
        x = x.astype(F32)
        return (x * c + pltpu.roll(x, HD // 2, axis=1) * s).astype(BF16)

    for h in range(HEADS):
        cols = slice(h * HD, (h + 1) * HD)
        kk_stage[h, :, 0:HD] = turned(k_ref[0, :, cols], cosine, sine)
        kk_stage[h, :, HD : 2 * HD] = turned(tk_ref[0, :, cols], cosine, sine)
    for load in loads[4:7]:
        load.wait()
    cosine, sine = cosine * 0.0625, sine * 0.0625
    for h in range(HEADS):
        cols = slice(h * HD, (h + 1) * HD)
        qq_stage[h, :, 0:HD] = turned(tq_ref[0, :, cols], cosine, sine)
        qq_stage[h, :, HD : 2 * HD] = turned(q_ref[0, :, cols], cosine, sine)
    id_stage[...] = jnp.broadcast_to(ids_ref[...].astype(F32), (8, HD))

    pl.semaphore_wait(barrier, n_ctx - 1 + n_dp - 1)

    rows_here = pl.ds(pl.multiple_of(me * ROWS, ROWS), ROWS)

    def pieces(h):
        cols = pl.ds(pl.multiple_of(h * HD, HD), HD)
        return [
            (id_stage, id_rows.at[me], send_id.at[h], recv_id),
            (kk_stage.at[h], kk.at[rows_here, :], send_k.at[h], recv_k),
            (v_ref.at[0, :, cols], vv.at[rows_here, pl.ds(0, HD)], send_v.at[h], recv_v),
            (tv_ref.at[0, :, cols], vv.at[rows_here, pl.ds(HD, HD)], send_tv.at[h], recv_v),
            (qq_stage.at[h], qq.at[rows_here, :], send_q.at[h], recv_q.at[me]),
        ]

    def remote(piece, to):
        src, dst, ssem, rsem = piece
        return pltpu.make_async_remote_copy(
            src_ref=src,
            dst_ref=dst,
            send_sem=ssem,
            recv_sem=rsem,
            device_id={"ctx": to},
            device_id_type=MESH,
        )

    def start_sends(which):
        @pl.loop(0, HEADS)
        def _(i):
            h = (i + my_head) % HEADS
            to = owner_of(h)

            @pl.when(to != me)
            def _():
                for p in which:
                    remote(pieces(h)[p], to).start()

            @pl.when(to == me)
            def _():
                for p in which:
                    src, dst, _, rsem = pieces(h)[p]
                    pltpu.make_async_copy(src, dst, rsem).start()

    start_sends((0, 1, 2, 3))
    start_sends((4,))

    @pl.when(is_owner)
    def _():
        pltpu.make_async_copy(id_rows, id_rows, recv_id).wait()

        @pl.loop(0, n_ctx)
        def _(j):
            ids = jnp.broadcast_to(id_rows[j, 0:1, :], (ROWS, HD))
            id_cols[pl.ds(pl.multiple_of(j * ROWS, ROWS), ROWS), :] = ids.T

        v_ones[:, HD : 2 * HD] = jnp.ones((n_ctx * ROWS, HD), BF16)
        pltpu.make_async_copy(kk, kk, recv_k).wait()
        pltpu.make_async_copy(vv, vv, recv_v).wait()
        v_ones[:, 0:HD] = vv[:, 0:HD]

        tile = 2 * ROWS
        step = math.log2(math.e) * math.sqrt(2.0)
        contract_last = (((1,), (1,)), ((), ()))

        @pl.loop(0, chips)
        def _(t):
            at = (chip + 2 * chips - 1 - t) % chips
            rows = pl.ds(pl.multiple_of(at * tile, tile), tile)
            for c in range(2):
                block = at * 2 + c
                part = qq.at[pl.ds(pl.multiple_of(block * ROWS, ROWS), ROWS), :]
                pltpu.make_async_copy(part, part, recv_q.at[block]).wait()
            both = qq[rows, :]
            q = both[:, HD : 2 * HD]
            mine = id_cols[rows, :]
            best = jnp.full((tile, HD), -jnp.inf, F32)
            for c in range(chips):
                keys = kk[c * tile : (c + 1) * tile, 0:HD]
                s = lax.dot_general(q, keys, contract_last, preferred_element_type=F32)
                for half in range(2):
                    j = 2 * c + half
                    theirs = jnp.broadcast_to(id_rows[j, 0:1, :], (tile, HD))
                    s_half = jnp.where(mine == theirs, s[:, half * HD : (half + 1) * HD], -jnp.inf)
                    s_buf[:, j * HD : (j + 1) * HD] = s_half
                    best = jnp.maximum(best, s_half)
            best = jnp.broadcast_to(jnp.max(best, axis=1, keepdims=True), (tile, HD))
            total = jnp.zeros((tile, HD), F32)
            for c in range(chips):
                keys = kk[c * tile : (c + 1) * tile, :]
                slopes = lax.dot_general(both, keys, contract_last, preferred_element_type=F32)
                for half in range(2):
                    j = 2 * c + half
                    there = slice(j * HD, (j + 1) * HD)
                    w = jnp.exp2((s_buf[:, there] - best) * step)
                    tilted = w * slopes[:, half * HD : (half + 1) * HD]
                    total = total + w
                    wb_buf[:, there] = w.astype(BF16)
                    tb_buf[:, there] = tilted.astype(BF16)
            sums = jnp.dot(wb_buf[...], vv[...], preferred_element_type=F32)
            tilted_sums = jnp.dot(tb_buf[...], v_ones[...], preferred_element_type=F32)
            slope_part = tilted_sums[:, 0:HD]
            total = jnp.sum(total, axis=1, keepdims=True)
            weighted = tilted_sums[:, HD : 2 * HD] * math.sqrt(2.0)
            primal, spread = sums[:, 0:HD], sums[:, HD : 2 * HD]
            result = (slope_part * math.sqrt(2.0) + spread) / total - (weighted / total) * (
                primal / total
            )
            out_stage[at] = result.astype(BF16)
            for c in range(2):
                block = at * 2 + c
                src = out_stage.at[at, pl.ds(c * ROWS, ROWS), :]
                dst = attn.at[:, pl.ds(pl.multiple_of(my_head * HD, HD), HD)]

                @pl.when(block != me)
                def _():
                    remote((src, dst, send_out.at[block], recv_out), block).start()

                @pl.when(block == me)
                def _():
                    pltpu.make_async_copy(src, dst, recv_out).start()

    for load in loads[7:]:
        load.wait()
    pltpu.make_async_copy(attn, attn, recv_out).wait()

    width = w_buf.shape[1]
    wide = width // 8
    for n in range(8):
        cols = slice(n * wide, (n + 1) * wide)
        projected = jnp.dot(attn[...], w_buf[:, cols], preferred_element_type=F32)
        branch_ref[0, :, cols] = (ls_ref[:, cols] * projected).astype(BF16)
        weighed = cot_ref[0, :, cols].astype(F32) * projected
        g_part[n : n + 1, :] = jnp.sum(weighed, axis=0, keepdims=True).astype(BF16)

    def exchange(axis, index, size, src, dst, ssem, rsem):
        def copy_to(i):
            return pltpu.make_async_remote_copy(
                src_ref=src,
                dst_ref=dst.at[index],
                send_sem=ssem.at[i],
                recv_sem=rsem,
                device_id={axis: (index + i) % size},
                device_id_type=MESH,
            )

        @pl.loop(1, size)
        def _(i):
            copy_to(i).start()

        pltpu.make_async_copy(src, dst.at[index], rsem).start()
        pltpu.make_async_copy(dst, dst, rsem).wait()
        return copy_to

    copy_c = exchange("ctx", me, n_ctx, g_part, g_ctx, send_gc, recv_gc)
    acc = g_ctx[0].astype(F32)
    for i in range(1, n_ctx):
        acc = acc + g_ctx[i].astype(F32)
    g_sum[...] = acc.astype(BF16)
    copy_d = exchange("dp", me_dp, n_dp, g_sum, g_dp, send_gd, recv_gd)
    acc = g_dp[0].astype(F32)
    for i in range(1, n_dp):
        acc = acc + g_dp[i].astype(F32)
    acc = acc / math.sqrt(n_ctx * n_dp * ROWS)
    for n in range(8):
        for c in range(wide // HD):
            at = n * (wide // HD) + c
            grad_ref[at : at + 1, :] = acc[n : n + 1, c * HD : (c + 1) * HD]

    @pl.loop(0, HEADS)
    def _(h):
        to = owner_of(h)

        @pl.when(to != me)
        def _():
            for piece in pieces(h):
                remote(piece, to).wait_send()

    @pl.when(is_owner)
    def _():
        @pl.loop(0, n_ctx)
        def _(block):
            @pl.when(block != me)
            def _():
                src = out_stage.at[block // 2, pl.ds((block % 2) * ROWS, ROWS), :]
                dst = attn.at[:, pl.ds(pl.multiple_of(my_head * HD, HD), HD)]
                remote((src, dst, send_out.at[block], recv_out), block).wait_send()

    @pl.loop(1, n_ctx)
    def _(i):
        copy_c(i).wait_send()

    @pl.loop(1, n_dp)
    def _(i):
        copy_d(i).wait_send()


def turn_tables(blocks):
    frequency = 10000.0 ** (-np.arange(HD // 2, dtype=np.float64) / (HD // 2))
    frequency = np.concatenate([frequency, frequency])
    inside = np.arange(ROWS, dtype=np.float64)[:, None] * frequency
    start = ROWS * np.arange(blocks, dtype=np.float64)[:, None] * frequency
    angles = np.concatenate([inside, start])
    return np.stack([np.cos(angles), np.sin(angles)]).astype(np.float32)


def solution(mesh):
    n_ctx, n_dp = mesh.shape["ctx"], mesh.shape["dp"]
    turns = turn_tables(n_ctx)

    def local(
        queries,
        keys,
        values,
        tangent_queries,
        tangent_keys,
        tangent_values,
        clip_ids,
        block_order,
        out_weight,
        layer_scale,
        cotangent,
    ):
        width = out_weight.shape[1]
        seq = n_ctx * ROWS
        tile = 2 * ROWS
        vmem = pl.BlockSpec(memory_space=pltpu.VMEM)
        dma = pltpu.SemaphoreType.DMA
        branch, grad = pl.pallas_call(
            lambda *refs: kernel(n_ctx, n_dp, *refs),
            out_shape=(
                jax.ShapeDtypeStruct((1, ROWS, width), BF16),
                jax.ShapeDtypeStruct((width // HD, HD), F32),
            ),
            in_specs=[pl.BlockSpec(memory_space=pltpu.HBM)] * 12,
            out_specs=(vmem, vmem),
            scratch_shapes=[
                pltpu.SMEM((n_ctx,), jnp.int32),
                pltpu.VMEM((1, ROWS, HEADS * HD), BF16),
                pltpu.VMEM((1, ROWS, HEADS * HD), BF16),
                pltpu.VMEM((1, ROWS, HEADS * HD), BF16),
                pltpu.VMEM((1, ROWS, HEADS * HD), BF16),
                pltpu.VMEM((1, ROWS), jnp.int32),
                pltpu.VMEM((2, ROWS + n_ctx, HD), F32),
                pltpu.VMEM((1, width), F32),
                pltpu.VMEM((1, ROWS, width), BF16),
                pltpu.VMEM((HEADS, ROWS, 2 * HD), BF16),
                pltpu.VMEM((HEADS, ROWS, 2 * HD), BF16),
                pltpu.VMEM((8, HD), F32),
                pltpu.VMEM((seq, 2 * HD), BF16),
                pltpu.VMEM((seq, 2 * HD), BF16),
                pltpu.VMEM((seq, 2 * HD), BF16),
                pltpu.VMEM((n_ctx, 8, HD), F32),
                pltpu.VMEM((seq, HD), F32),
                pltpu.VMEM((tile, seq), F32),
                pltpu.VMEM((tile, seq), BF16),
                pltpu.VMEM((tile, seq), BF16),
                pltpu.VMEM((seq, 2 * HD), BF16),
                pltpu.VMEM((n_ctx // 2, tile, HD), BF16),
                pltpu.VMEM((ROWS, HEADS * HD), BF16),
                pltpu.VMEM((HEADS * HD, width), BF16),
                pltpu.VMEM((8, width // 8), BF16),
                pltpu.VMEM((n_ctx, 8, width // 8), BF16),
                pltpu.VMEM((8, width // 8), BF16),
                pltpu.VMEM((n_dp, 8, width // 8), BF16),
                dma((10,)),
                dma((HEADS,)),
                dma((HEADS,)),
                dma((HEADS,)),
                dma((HEADS,)),
                dma((HEADS,)),
                dma,
                dma,
                dma((n_ctx,)),
                dma,
                dma((n_ctx,)),
                dma,
                dma((n_ctx,)),
                dma,
                dma((n_dp,)),
                dma,
            ],
            compiler_params=pltpu.CompilerParams(
                collective_id=0,
                has_side_effects=True,
                vmem_limit_bytes=48 * 1024 * 1024,
            ),
        )(
            *[pltpu.with_memory_space_constraint(x, pltpu.HBM) for x in (
                block_order,
                queries,
                keys,
                values,
                tangent_queries,
                tangent_keys,
                tangent_values,
                clip_ids,
                jnp.asarray(turns),
                out_weight,
                layer_scale.reshape(1, width),
                cotangent,
            )]
        )
        return branch, grad.reshape(width)

    tokens = P("dp", "ctx", None)
    in_specs = (tokens,) * 6 + (P("dp", "ctx"), P(), P(), P(), tokens)
    return jax.shard_map(
        local, mesh=mesh, in_specs=in_specs, out_specs=(tokens, P()), check_vma=False
    )
```

```python
import math

import jax
import jax.numpy as jnp
import numpy as np
from jax import lax
from jax.experimental import pallas as pl
from jax.experimental.pallas import tpu as pltpu
from jax.sharding import PartitionSpec as P

MESH = pl.DeviceIdType.MESH
HEADS = 12
HD = 128
ROWS = 128
F32 = jnp.float32
BF16 = jnp.bfloat16


def owner_of(head):
    row, rest = head // 6, head % 6
    return 8 * row + rest + (rest + 2 * row) // 3


def kernel(
    n_ctx,
    n_dp,
    order_hbm,
    q_hbm,
    k_hbm,
    v_ref,
    tq_hbm,
    tk_hbm,
    tv_ref,
    ids_hbm,
    turn_hbm,
    w_hbm,
    ls_hbm,
    cot_hbm,
    branch_ref,
    grad_ref,
    order_ref,
    q_ref,
    k_ref,
    tq_ref,
    tk_ref,
    ids_ref,
    turn_ref,
    ls_ref,
    cot_ref,
    kk_stage,
    qq_stage,
    id_stage,
    kk,
    vv,
    qq,
    id_rows,
    id_cols,
    s_buf,
    wb_buf,
    tb_buf,
    v_ones,
    out_stage,
    attn,
    w_buf,
    g_part,
    g_ctx,
    g_sum,
    g_dp,
    load_sem,
    send_k,
    send_v,
    send_tv,
    send_q,
    send_id,
    recv_k,
    recv_v,
    recv_q,
    recv_id,
    send_out,
    recv_out,
    send_gc,
    recv_gc,
    send_gd,
    recv_gd,
):
    me = lax.axis_index("ctx")
    me_dp = lax.axis_index("dp")
    chip, core = me // 2, me % 2
    row, col = chip // 4, chip % 4
    my_head = 6 * row + (3 * col + 1 - row) // 2 + core
    is_owner = core * ((row + col) % 2) == 0
    chips = n_ctx // 2

    barrier = pltpu.get_barrier_semaphore()

    @pl.loop(1, n_ctx)
    def _(i):
        pl.semaphore_signal(
            barrier, inc=1, device_id={"ctx": (me + i) % n_ctx}, device_id_type=MESH
        )

    @pl.loop(1, n_dp)
    def _(i):
        pl.semaphore_signal(
            barrier, inc=1, device_id={"dp": (me_dp + i) % n_dp}, device_id_type=MESH
        )

    loads = [
        pltpu.make_async_copy(src, dst, load_sem.at[i])
        for i, (src, dst) in enumerate(
            [
                (order_hbm, order_ref),
                (turn_hbm, turn_ref),
                (k_hbm, k_ref),
                (tk_hbm, tk_ref),
                (q_hbm, q_ref),
                (tq_hbm, tq_ref),
                (ids_hbm, ids_ref),
                (ls_hbm, ls_ref),
                (cot_hbm, cot_ref),
                (w_hbm, w_buf),
            ]
        )
    ]
    for load in loads:
        load.start()

    for load in loads[:4]:
        load.wait()
    place = order_ref[me]
    cos_b = turn_ref[0, pl.ds(ROWS + place, 1), :]
    sin_b = turn_ref[1, pl.ds(ROWS + place, 1), :]
    cos_t, sin_t = turn_ref[0, 0:ROWS, :], turn_ref[1, 0:ROWS, :]
    lane = lax.broadcasted_iota(jnp.int32, (ROWS, HD), 1)
    cosine = cos_b * cos_t - sin_b * sin_t
    sine = sin_b * cos_t + cos_b * sin_t
    sine = jnp.where(lane < HD // 2, -sine, sine)

    def turned(x, c, s):
        x = x.astype(F32)
        return (x * c + pltpu.roll(x, HD // 2, axis=1) * s).astype(BF16)

    for h in range(HEADS):
        cols = slice(h * HD, (h + 1) * HD)
        kk_stage[h, :, 0:HD] = turned(k_ref[0, :, cols], cosine, sine)
        kk_stage[h, :, HD : 2 * HD] = turned(tk_ref[0, :, cols], cosine, sine)
    for load in loads[4:7]:
        load.wait()
    cosine, sine = cosine * 0.0625, sine * 0.0625
    for h in range(HEADS):
        cols = slice(h * HD, (h + 1) * HD)
        qq_stage[h, :, 0:HD] = turned(tq_ref[0, :, cols], cosine, sine)
        qq_stage[h, :, HD : 2 * HD] = turned(q_ref[0, :, cols], cosine, sine)
    id_stage[...] = jnp.broadcast_to(ids_ref[...].astype(F32), (8, HD))

    pl.semaphore_wait(barrier, n_ctx - 1 + n_dp - 1)

    rows_here = pl.ds(pl.multiple_of(me * ROWS, ROWS), ROWS)

    def pieces(h):
        cols = pl.ds(pl.multiple_of(h * HD, HD), HD)
        return [
            (id_stage, id_rows.at[me], send_id.at[h], recv_id),
            (kk_stage.at[h], kk.at[rows_here, :], send_k.at[h], recv_k),
            (v_ref.at[0, :, cols], vv.at[rows_here, pl.ds(0, HD)], send_v.at[h], recv_v),
            (tv_ref.at[0, :, cols], vv.at[rows_here, pl.ds(HD, HD)], send_tv.at[h], recv_v),
            (qq_stage.at[h], qq.at[rows_here, :], send_q.at[h], recv_q.at[me]),
        ]

    def remote(piece, to):
        src, dst, ssem, rsem = piece
        return pltpu.make_async_remote_copy(
            src_ref=src,
            dst_ref=dst,
            send_sem=ssem,
            recv_sem=rsem,
            device_id={"ctx": to},
            device_id_type=MESH,
        )

    def start_sends(which):
        @pl.loop(0, HEADS)
        def _(i):
            h = (i + my_head) % HEADS
            to = owner_of(h)

            @pl.when(to != me)
            def _():
                for p in which:
                    remote(pieces(h)[p], to).start()

            @pl.when(to == me)
            def _():
                for p in which:
                    src, dst, _, rsem = pieces(h)[p]
                    pltpu.make_async_copy(src, dst, rsem).start()

    start_sends((0, 1, 4, 2, 3))

    @pl.when(is_owner)
    def _():
        pltpu.make_async_copy(id_rows, id_rows, recv_id).wait()

        @pl.loop(0, n_ctx)
        def _(j):
            ids = jnp.broadcast_to(id_rows[j, 0:1, :], (ROWS, HD))
            id_cols[pl.ds(pl.multiple_of(j * ROWS, ROWS), ROWS), :] = ids.T

        v_ones[:, HD : 2 * HD] = jnp.ones((n_ctx * ROWS, HD), BF16)
        pltpu.make_async_copy(kk, kk, recv_k).wait()
        pltpu.make_async_copy(vv, vv, recv_v).wait()
        v_ones[:, 0:HD] = vv[:, 0:HD]

        tile = 2 * ROWS
        step = math.log2(math.e) * math.sqrt(2.0)
        contract_last = (((1,), (1,)), ((), ()))

        @pl.loop(0, chips)
        def _(t):
            at = (chip + 2 * chips - 1 - t) % chips
            rows = pl.ds(pl.multiple_of(at * tile, tile), tile)
            for c in range(2):
                block = at * 2 + c
                part = qq.at[pl.ds(pl.multiple_of(block * ROWS, ROWS), ROWS), :]
                pltpu.make_async_copy(part, part, recv_q.at[block]).wait()
            both = qq[rows, :]
            q = both[:, HD : 2 * HD]
            mine = id_cols[rows, :]
            best = jnp.full((tile, HD), -jnp.inf, F32)
            for c in range(chips):
                keys = kk[c * tile : (c + 1) * tile, 0:HD]
                s = lax.dot_general(q, keys, contract_last, preferred_element_type=F32)
                for half in range(2):
                    j = 2 * c + half
                    theirs = jnp.broadcast_to(id_rows[j, 0:1, :], (tile, HD))
                    s_half = jnp.where(mine == theirs, s[:, half * HD : (half + 1) * HD], -jnp.inf)
                    s_buf[:, j * HD : (j + 1) * HD] = s_half
                    best = jnp.maximum(best, s_half)
            best = jnp.broadcast_to(jnp.max(best, axis=1, keepdims=True), (tile, HD))
            total = jnp.zeros((tile, HD), F32)
            for c in range(chips):
                keys = kk[c * tile : (c + 1) * tile, :]
                slopes = lax.dot_general(both, keys, contract_last, preferred_element_type=F32)
                for half in range(2):
                    j = 2 * c + half
                    there = slice(j * HD, (j + 1) * HD)
                    w = jnp.exp2((s_buf[:, there] - best) * step)
                    tilted = w * slopes[:, half * HD : (half + 1) * HD]
                    total = total + w
                    wb_buf[:, there] = w.astype(BF16)
                    tb_buf[:, there] = tilted.astype(BF16)
            sums = jnp.dot(wb_buf[...], vv[...], preferred_element_type=F32)
            tilted_sums = jnp.dot(tb_buf[...], v_ones[...], preferred_element_type=F32)
            slope_part = tilted_sums[:, 0:HD]
            total = jnp.sum(total, axis=1, keepdims=True)
            weighted = tilted_sums[:, HD : 2 * HD] * math.sqrt(2.0)
            primal, spread = sums[:, 0:HD], sums[:, HD : 2 * HD]
            result = (slope_part * math.sqrt(2.0) + spread) / total - (weighted / total) * (
                primal / total
            )
            out_stage[at] = result.astype(BF16)
            for c in range(2):
                block = at * 2 + c
                src = out_stage.at[at, pl.ds(c * ROWS, ROWS), :]
                dst = attn.at[:, pl.ds(pl.multiple_of(my_head * HD, HD), HD)]

                @pl.when(block != me)
                def _():
                    remote((src, dst, send_out.at[block], recv_out), block).start()

                @pl.when(block == me)
                def _():
                    pltpu.make_async_copy(src, dst, recv_out).start()

    for load in loads[7:]:
        load.wait()
    pltpu.make_async_copy(attn, attn, recv_out).wait()

    width = w_buf.shape[1]
    wide = width // 8
    for n in range(8):
        cols = slice(n * wide, (n + 1) * wide)
        projected = jnp.dot(attn[...], w_buf[:, cols], preferred_element_type=F32)
        branch_ref[0, :, cols] = (ls_ref[:, cols] * projected).astype(BF16)
        weighed = cot_ref[0, :, cols].astype(F32) * projected
        g_part[n : n + 1, :] = jnp.sum(weighed, axis=0, keepdims=True).astype(BF16)

    def exchange(axis, index, size, src, dst, ssem, rsem):
        def copy_to(i):
            return pltpu.make_async_remote_copy(
                src_ref=src,
                dst_ref=dst.at[index],
                send_sem=ssem.at[i],
                recv_sem=rsem,
                device_id={axis: (index + i) % size},
                device_id_type=MESH,
            )

        @pl.loop(1, size)
        def _(i):
            copy_to(i).start()

        pltpu.make_async_copy(src, dst.at[index], rsem).start()
        pltpu.make_async_copy(dst, dst, rsem).wait()
        return copy_to

    copy_c = exchange("ctx", me, n_ctx, g_part, g_ctx, send_gc, recv_gc)
    acc = g_ctx[0].astype(F32)
    for i in range(1, n_ctx):
        acc = acc + g_ctx[i].astype(F32)
    g_sum[...] = acc.astype(BF16)
    copy_d = exchange("dp", me_dp, n_dp, g_sum, g_dp, send_gd, recv_gd)
    acc = g_dp[0].astype(F32)
    for i in range(1, n_dp):
        acc = acc + g_dp[i].astype(F32)
    acc = acc / math.sqrt(n_ctx * n_dp * ROWS)
    for n in range(8):
        for c in range(wide // HD):
            at = n * (wide // HD) + c
            grad_ref[at : at + 1, :] = acc[n : n + 1, c * HD : (c + 1) * HD]

    @pl.loop(0, HEADS)
    def _(h):
        to = owner_of(h)

        @pl.when(to != me)
        def _():
            for piece in pieces(h):
                remote(piece, to).wait_send()

    @pl.when(is_owner)
    def _():
        @pl.loop(0, n_ctx)
        def _(block):
            @pl.when(block != me)
            def _():
                src = out_stage.at[block // 2, pl.ds((block % 2) * ROWS, ROWS), :]
                dst = attn.at[:, pl.ds(pl.multiple_of(my_head * HD, HD), HD)]
                remote((src, dst, send_out.at[block], recv_out), block).wait_send()

    @pl.loop(1, n_ctx)
    def _(i):
        copy_c(i).wait_send()

    @pl.loop(1, n_dp)
    def _(i):
        copy_d(i).wait_send()


def turn_tables(blocks):
    frequency = 10000.0 ** (-np.arange(HD // 2, dtype=np.float64) / (HD // 2))
    frequency = np.concatenate([frequency, frequency])
    inside = np.arange(ROWS, dtype=np.float64)[:, None] * frequency
    start = ROWS * np.arange(blocks, dtype=np.float64)[:, None] * frequency
    angles = np.concatenate([inside, start])
    return np.stack([np.cos(angles), np.sin(angles)]).astype(np.float32)


def solution(mesh):
    n_ctx, n_dp = mesh.shape["ctx"], mesh.shape["dp"]
    turns = turn_tables(n_ctx)

    def local(
        queries,
        keys,
        values,
        tangent_queries,
        tangent_keys,
        tangent_values,
        clip_ids,
        block_order,
        out_weight,
        layer_scale,
        cotangent,
    ):
        width = out_weight.shape[1]
        seq = n_ctx * ROWS
        tile = 2 * ROWS
        vmem = pl.BlockSpec(memory_space=pltpu.VMEM)
        dma = pltpu.SemaphoreType.DMA
        branch, grad = pl.pallas_call(
            lambda *refs: kernel(n_ctx, n_dp, *refs),
            out_shape=(
                jax.ShapeDtypeStruct((1, ROWS, width), BF16),
                jax.ShapeDtypeStruct((width // HD, HD), F32),
            ),
            in_specs=[pl.BlockSpec(memory_space=pltpu.HBM)] * 12,
            out_specs=(vmem, vmem),
            scratch_shapes=[
                pltpu.SMEM((n_ctx,), jnp.int32),
                pltpu.VMEM((1, ROWS, HEADS * HD), BF16),
                pltpu.VMEM((1, ROWS, HEADS * HD), BF16),
                pltpu.VMEM((1, ROWS, HEADS * HD), BF16),
                pltpu.VMEM((1, ROWS, HEADS * HD), BF16),
                pltpu.VMEM((1, ROWS), jnp.int32),
                pltpu.VMEM((2, ROWS + n_ctx, HD), F32),
                pltpu.VMEM((1, width), F32),
                pltpu.VMEM((1, ROWS, width), BF16),
                pltpu.VMEM((HEADS, ROWS, 2 * HD), BF16),
                pltpu.VMEM((HEADS, ROWS, 2 * HD), BF16),
                pltpu.VMEM((8, HD), F32),
                pltpu.VMEM((seq, 2 * HD), BF16),
                pltpu.VMEM((seq, 2 * HD), BF16),
                pltpu.VMEM((seq, 2 * HD), BF16),
                pltpu.VMEM((n_ctx, 8, HD), F32),
                pltpu.VMEM((seq, HD), F32),
                pltpu.VMEM((tile, seq), F32),
                pltpu.VMEM((tile, seq), BF16),
                pltpu.VMEM((tile, seq), BF16),
                pltpu.VMEM((seq, 2 * HD), BF16),
                pltpu.VMEM((n_ctx // 2, tile, HD), BF16),
                pltpu.VMEM((ROWS, HEADS * HD), BF16),
                pltpu.VMEM((HEADS * HD, width), BF16),
                pltpu.VMEM((8, width // 8), BF16),
                pltpu.VMEM((n_ctx, 8, width // 8), BF16),
                pltpu.VMEM((8, width // 8), BF16),
                pltpu.VMEM((n_dp, 8, width // 8), BF16),
                dma((10,)),
                dma((HEADS,)),
                dma((HEADS,)),
                dma((HEADS,)),
                dma((HEADS,)),
                dma((HEADS,)),
                dma,
                dma,
                dma((n_ctx,)),
                dma,
                dma((n_ctx,)),
                dma,
                dma((n_ctx,)),
                dma,
                dma((n_dp,)),
                dma,
            ],
            compiler_params=pltpu.CompilerParams(
                collective_id=0,
                has_side_effects=True,
                vmem_limit_bytes=48 * 1024 * 1024,
            ),
        )(
            *[pltpu.with_memory_space_constraint(x, pltpu.HBM) for x in (
                block_order,
                queries,
                keys,
                values,
                tangent_queries,
                tangent_keys,
                tangent_values,
                clip_ids,
                jnp.asarray(turns),
                out_weight,
                layer_scale.reshape(1, width),
                cotangent,
            )]
        )
        return branch, grad.reshape(width)

    tokens = P("dp", "ctx", None)
    in_specs = (tokens,) * 6 + (P("dp", "ctx"), P(), P(), P(), tokens)
    return jax.shard_map(
        local, mesh=mesh, in_specs=in_specs, out_specs=(tokens, P()), check_vma=False
    )
```
